32 devices in a mesh: grp: 2 (over x), pi: 16 (over z, y, core).
Axes of the slice: x: 2, y: 2, z: 4, core: 2. Of those that a mesh axis runs over, the one named last changes fastest.
Arguments:
- left: bfloat16 [128, 1024], P(('grp', 'pi')), parts along dimension 0, may hold values from -6 to 6
- right: bfloat16 [128, 1024], P(('grp', 'pi')), parts along dimension 0, may hold values from -6 to 6
- depth: int32 [128], P(('grp', 'pi')), parts along dimension 0, may hold values from 1 to 32
- w_out: bfloat16 [1024, 128], replicated, may hold values from -0.1875 to 0.1875
- bias: float32 [128], replicated, may hold values from -4 to 4
- pair_cot: bfloat16 [128, 64, 128], P(('grp', 'pi')), parts along dimension 0, may hold values from -6 to 6
Outputs:
- pair_update: bfloat16 [128, 64, 128], P(('grp', 'pi')), parts along dimension 0
- grad_left: float32 [128, 1024], P(('grp', 'pi')), parts along dimension 0
- grad_right: float32 [128, 1024], P(('grp', 'pi')), parts along dimension 0
- grad_w: float32 [2048, 128], P('grp'), parts along dimension 0
- grad_bias: float32 [256], P('grp'), parts along dimension 0
The draws below stay inside these ranges and needn't reach their ends.
There are 2 independent parts, one for each index of `grp`. The reference program is written for one: setup_inputs(seed, part) draws one part's arguments, and reference() takes and returns one part's arrays. A program takes and returns all parts, laid end to end along the dimension named above; an argument that names none is the same for every part. Nothing has to cross between parts.
All inputs are finite; a program needn't handle non-finite values.
Results may differ from the reference program's by a relative error of at most 0.0034.
Values may be sent and summed in bfloat16 or wider, within the bound.
A program may use at most 64 MiB of HBM per device.

```python
import math
import jax
import jax.numpy as jnp
from jax import lax

C = 32
CZ = 128
ROWS = 32
N = 64


def with_ends(drawn, key, least, largest):
    longest = drawn.shape.index(max(drawn.shape))
    spots = []
    for shift in (0, 1):
        where = [jax.random.randint(jax.random.fold_in(key, axis), (), 0, length) for axis, length in enumerate(drawn.shape)]
        where[longest] = (where[longest] + shift) % drawn.shape[longest]
        spots.append(tuple(where))
    return drawn.at[spots[0]].set(least).at[spots[1]].set(largest)


def raised(drawn, stream_key, source, target, shards_of, factor):
    def block_of(axis_at):
        return (jnp.arange(drawn.shape[axis_at]) // (drawn.shape[axis_at] // shards_of)).reshape((-1,) + (1,) * (drawn.ndim - 1 - axis_at))

    first = jax.random.permutation(stream_key, shards_of)[block_of(target)]
    second = (block_of(target) + shards_of // 2) % shards_of
    return jnp.where((block_of(source) == first) | (block_of(source) == second), factor * drawn, drawn)


def levels(stream_key, extent, pieces, smallest, high):
    gain = 1.0
    for dim, blocks in pieces:
        draws = jax.random.uniform(jax.random.fold_in(jax.random.fold_in(stream_key, 6), dim), (blocks,), jnp.float32, smallest / len(pieces), high / len(pieces))
        gain = gain * jnp.repeat(jnp.exp(draws), extent[dim] // blocks).reshape((-1,) + (1,) * (len(extent) - 1 - dim))
    return gain


def bell_draw(own_key, extent, width, most, split=(), held_as=jnp.bfloat16):
    drawn = jax.random.normal(own_key, extent, jnp.float32) * width
    if len(split) > 0:
        drawn = levels(own_key, extent, split, -0.22, 0.18) * drawn
    return jnp.clip(drawn, min=-most, max=most).astype(held_as)


def noise_with(rng, extent, scale, reach, shards, heavy, kind=jnp.bfloat16):
    entries = scale * jax.random.normal(rng, extent, jnp.float32)
    if shards:
        entries = entries * levels(rng, extent, shards, -0.22, 0.18)
    return jnp.clip(raised(entries, jax.random.fold_in(rng, 3), *heavy), -reach, reach).astype(kind)


def setup_inputs(seed: int = 0, part: int = 0) -> dict:
    arg_keys = jax.random.split(jax.random.key(seed), 7)
    part_splits = jax.random.split(jax.random.fold_in(arg_keys[6], part), 7)
    return {
        "left": bell_draw(part_splits[0], (N, ROWS * C), 1.0, 6.0, ((0, 16),)),
        "right": bell_draw(part_splits[1], (N, ROWS * C), 1.0, 6.0, ((0, 16),)),
        "depth": with_ends(jax.random.randint(part_splits[2], (N,), 1, ROWS + 1), jax.random.fold_in(part_splits[2], 1), 1, ROWS).astype(jnp.int32),
        "w_out": bell_draw(arg_keys[3], (C * C, CZ), (C * C) ** -0.5, 0.1875),
        "bias": bell_draw(arg_keys[4], (CZ,), 1.0, 4.0, (), jnp.float32),
        "pair_cot": noise_with(part_splits[5], (N, N, CZ), 1.0, 6.0, ((0, 16),), (0, 1, 16, 2.0)),
    }


epsilon = 1e-3


def reference(left, right, depth, w_out, bias, pair_cot):
    row_ids = jnp.arange(ROWS, dtype=jnp.int32)
    mask = (row_ids[None, :] < depth[:, None]).astype(jnp.bfloat16)
    left_masked = left.reshape(N, ROWS, C) * mask[:, :, None]
    right_masked = right.reshape(N, ROWS, C) * mask[:, :, None]
    block = math.gcd(N, 32)
    blocks = N // block

    def one_block(carry, block_index):
        weight_acc, bias_acc, right_acc = carry
        begin = (block_index * block).astype(jnp.int32)
        left_block = lax.dynamic_slice_in_dim(left_masked, begin, block, 0)
        depth_block = lax.dynamic_slice_in_dim(depth, begin, block, 0)
        mask_block = lax.dynamic_slice_in_dim(mask, begin, block, 0)
        cot_block = lax.dynamic_slice_in_dim(pair_cot, begin, block, 0)
        count = epsilon + jnp.minimum(depth_block[:, None], depth[None, :]).astype(jnp.float32)
        outer = jnp.einsum("isc,jsd->ijcd", left_block.astype(jnp.float32), right_masked.astype(jnp.float32))
        outer = (outer / count[:, :, None, None]).reshape(block, N, C * C).astype(jnp.bfloat16)
        update = (jnp.dot(outer, w_out, preferred_element_type=jnp.float32) + bias).astype(jnp.bfloat16)
        weight_acc = weight_acc + jnp.dot(outer.reshape(-1, C * C).T, cot_block.reshape(-1, CZ), preferred_element_type=jnp.float32)
        bias_acc = bias_acc + jnp.sum(cot_block, axis=(0, 1), dtype=jnp.float32)
        grad_pair = jnp.dot(cot_block, w_out.T, preferred_element_type=jnp.float32) / count[:, :, None]
        grad_pair = grad_pair.astype(jnp.bfloat16).reshape(block, N, C, C).astype(jnp.float32)
        left_grad = jnp.einsum("ijcd,jsd->isc", grad_pair, right_masked.astype(jnp.float32)) * mask_block[:, :, None]
        right_acc = right_acc + jnp.einsum("ijcd,isc->jsd", grad_pair, left_block.astype(jnp.float32))
        return (weight_acc, bias_acc, right_acc), (update, left_grad)

    init = (jnp.zeros((C * C, CZ), jnp.float32), jnp.zeros((CZ,), jnp.float32), jnp.zeros((N, ROWS, C), jnp.float32))
    carry, stacked = lax.scan(one_block, init, jnp.arange(blocks, dtype=jnp.int32))
    weight_acc, bias_acc, right_acc = carry
    updates, left_grads = stacked
    pair_update = updates.reshape(N, N, CZ)
    grad_left = left_grads.reshape(N, ROWS * C)
    grad_right = (right_acc * mask[:, :, None]).reshape(N, ROWS * C)
    return pair_update, grad_left, grad_right, weight_acc, bias_acc
```

```python
import functools

import jax
import jax.numpy as jnp
from jax import lax
from jax.experimental import pallas as pl
from jax.experimental.pallas import tpu as pltpu
from jax.sharding import PartitionSpec as P

C = 32
EPSILON = 0.001
EXTRA = 16
MESH = pl.DeviceIdType.MESH
F32 = jnp.float32
BF16 = jnp.bfloat16


def split(x):
    high = x.astype(BF16)
    return high, (x - high.astype(F32)).astype(BF16)


def mm(x, y):
    return jnp.dot(x, y, preferred_element_type=F32)


def mm_nt(x, y):
    return lax.dot_general(x, y, (((1,), (1,)), ((), ())), preferred_element_type=F32)


def kernel(
    n, x_ref, a_ref, cot_ref, w_ref, bias_ref,
    pu_ref, gl_ref, gr_ref, gw_ref, gb_ref,
    gat, bs, uhi, ulo, t_ref, send_w, recv_w, part_r, send_r, recv_r, mine_w, all_w,
    send_sems, recv_sems,
):
    me = lax.axis_index("pi")
    rows = x_ref.shape[0]
    z = w_ref.shape[1]
    width = x_ref.shape[1] - z
    samples = width // C
    total = cot_ref.shape[1]
    chunk = gw_ref.shape[1]

    def copy(k, source, target, peer, slot):
        return pltpu.make_async_remote_copy(
            src_ref=source, dst_ref=target.at[slot],
            send_sem=send_sems.at[k, peer], recv_sem=recv_sems.at[k, slot],
            device_id={"pi": peer}, device_id_type=MESH,
        )

    def each(act):
        def body(step, carry):
            act(lax.rem(me + step, n))
            return carry

        lax.fori_loop(1, n, body, 0)

    barrier = pltpu.get_barrier_semaphore()
    each(lambda p: pl.semaphore_signal(barrier, inc=1, device_id={"pi": p}, device_id_type=MESH))
    pl.semaphore_wait(barrier, n - 1)
    each(lambda p: copy(0, x_ref, gat, p, me).start())
    gat[me] = x_ref[...]

    a = a_ref[...]
    for d in range(C):
        high, low = split(mm(a, w_ref[d * C:(d + 1) * C, :]))
        for i in range(rows):
            here = (slice(d * samples, (d + 1) * samples), slice(i * z, (i + 1) * z))
            uhi[here] = high[i * samples:(i + 1) * samples]
            ulo[here] = low[i * samples:(i + 1) * samples]
    a_t = jnp.concatenate([a, a], axis=0).astype(F32).T.astype(BF16)

    each(lambda p: copy(0, x_ref, gat, p, p).wait_recv())

    def gather_rows(q, carry):
        both = jnp.concatenate([gat[2 * q].astype(F32), gat[2 * q + 1].astype(F32)], axis=0)
        bs[pl.ds(pl.multiple_of(q * 2 * rows, 2 * rows), 2 * rows), :] = both
        return carry

    lax.fori_loop(0, n // 2, gather_rows, 0)
    b32 = bs[:, :width]
    b = b32.astype(BF16)
    depths = bs[:, width:]
    inverse, highs, lows = [], [], []
    cot_sum = jnp.zeros((1, z), F32)
    for i in range(rows):
        inverse.append(1.0 / (EPSILON + jnp.minimum(depths, x_ref[i:i + 1, width:].astype(F32))))
        cot = cot_ref[i].astype(F32)
        cot_sum = cot_sum + jnp.sum(cot, axis=0, keepdims=True)
        high, low = split(cot * inverse[i])
        highs.append(high)
        lows.append(low)
    cot_high = jnp.concatenate(highs, axis=1)
    cot_low = jnp.concatenate(lows, axis=1)
    b_t = jnp.concatenate([b32, b32], axis=0).T.astype(BF16)
    t_ref[...] = mm(b_t, jnp.concatenate([cot_high, cot_low], axis=0))

    def t_of(d):
        return jnp.concatenate(
            [t_ref[d * samples:(d + 1) * samples, i * z:(i + 1) * z] for i in range(rows)], axis=0
        )

    sum_high, sum_low = split(cot_sum)
    per = max(1, chunk // C)
    for d in range(C):
        high, low = split(t_of(d))
        piece = mm(a_t, jnp.concatenate([high, low], axis=0)).astype(BF16)
        if chunk >= C:
            send_w[d // per, (d % per) * C:(d % per + 1) * C, :] = piece
        else:
            for k in range(C // chunk):
                send_w[d * (C // chunk) + k, :chunk, :] = piece[k * chunk:(k + 1) * chunk]
    sums = jnp.concatenate(
        [sum_high.astype(F32), sum_low.astype(F32), jnp.zeros((EXTRA - 2, z), F32)], axis=0
    ).astype(BF16)

    def put_sums(p, carry):
        send_w[p, chunk:, :] = sums
        return carry

    lax.fori_loop(0, n, put_sums, 0)
    each(lambda p: copy(1, send_w.at[p], recv_w, p, me).start())
    recv_w[me] = send_w[me]

    u_high = uhi[...]
    part_r[...] = mm_nt(cot_high, u_high) + mm_nt(cot_low, u_high) + mm_nt(cot_high, ulo[...])

    def scatter_rows(q, carry):
        both = part_r[pl.ds(pl.multiple_of(q * 2 * rows, 2 * rows), 2 * rows), :]
        send_r[2 * q] = both[:rows].astype(BF16)
        send_r[2 * q + 1] = both[rows:].astype(BF16)
        return carry

    lax.fori_loop(0, n // 2, scatter_rows, 0)
    each(lambda p: copy(2, send_r.at[p], recv_r, p, me).start())
    recv_r[me] = send_r[me]

    each(lambda p: copy(1, send_w.at[p], recv_w, p, p).wait_recv())

    def add_w(p, acc):
        return acc + recv_w[p].astype(F32)

    total_w = lax.fori_loop(0, n, add_w, jnp.zeros((chunk + EXTRA, z), F32))
    mine_w[...] = total_w[:chunk].astype(BF16)
    gb_ref[...] = total_w[chunk:chunk + 1] + total_w[chunk + 1:chunk + 2]
    each(lambda p: copy(3, mine_w, all_w, p, me).start())
    all_w[me] = mine_w[...]

    update = mm(b, u_high) + mm(b, ulo[...])
    for i in range(rows):
        pu_ref[i] = (update[:, i * z:(i + 1) * z] * inverse[i] + bias_ref[...]).astype(BF16)

    left_acc = jnp.zeros((rows * samples, C), F32)
    for d in range(C):
        high, low = split(t_of(d))
        w_d = w_ref[d * C:(d + 1) * C, :]
        left_acc = left_acc + mm_nt(
            jnp.concatenate([high, low], axis=1), jnp.concatenate([w_d, w_d], axis=1)
        )
    gl_ref[...] = left_acc

    each(lambda p: copy(2, send_r.at[p], recv_r, p, p).wait_recv())

    def add_r(p, acc):
        return acc + recv_r[p].astype(F32)

    gr_ref[...] = lax.fori_loop(0, n, add_r, jnp.zeros((rows, width), F32))

    each(lambda p: copy(3, mine_w, all_w, p, p).wait_recv())
    gw_ref[...] = all_w[...]
    each(lambda p: copy(0, x_ref, gat, p, me).wait_send())
    each(lambda p: copy(1, send_w.at[p], recv_w, p, me).wait_send())
    each(lambda p: copy(2, send_r.at[p], recv_r, p, me).wait_send())
    each(lambda p: copy(3, mine_w, all_w, p, me).wait_send())


def local(n, left, right, depth, w_out, bias, pair_cot):
    rows, width = left.shape
    samples = width // C
    total, z = pair_cot.shape[1:]
    chunk = w_out.shape[0] // n
    mask = jnp.arange(samples, dtype=jnp.int32)[None, :] < depth[:, None]
    own = mask.astype(BF16)[:, :, None]
    a = (left.reshape(rows, samples, C) * own).reshape(rows * samples, C)
    b = (right.reshape(rows, samples, C) * own).transpose(0, 2, 1).reshape(rows, width)
    x = jnp.concatenate([b, jnp.broadcast_to(depth.astype(BF16)[:, None], (rows, z))], axis=1)
    w = w_out.reshape(C, C, z).transpose(1, 0, 2).reshape(C * C, z)
    vmem = pl.BlockSpec(memory_space=pltpu.VMEM)
    pu, gl, gr, gw, gb = pl.pallas_call(
        functools.partial(kernel, n),
        out_shape=(
            jax.ShapeDtypeStruct((rows, total, z), BF16),
            jax.ShapeDtypeStruct((rows * samples, C), F32),
            jax.ShapeDtypeStruct((rows, width), F32),
            jax.ShapeDtypeStruct((n, chunk, z), BF16),
            jax.ShapeDtypeStruct((1, z), F32),
        ),
        in_specs=[vmem] * 5,
        out_specs=(vmem,) * 5,
        scratch_shapes=[
            pltpu.VMEM((n, rows, width + z), BF16),
            pltpu.VMEM((total, width + z), F32),
            pltpu.VMEM((C * samples, rows * z), BF16),
            pltpu.VMEM((C * samples, rows * z), BF16),
            pltpu.VMEM((C * samples, rows * z), F32),
            pltpu.VMEM((n, chunk + EXTRA, z), BF16),
            pltpu.VMEM((n, chunk + EXTRA, z), BF16),
            pltpu.VMEM((total, width), F32),
            pltpu.VMEM((n, rows, width), BF16),
            pltpu.VMEM((n, rows, width), BF16),
            pltpu.VMEM((chunk, z), BF16),
            pltpu.VMEM((n, chunk, z), BF16),
            pltpu.SemaphoreType.DMA((4, n)),
            pltpu.SemaphoreType.DMA((4, n)),
        ],
        compiler_params=pltpu.CompilerParams(collective_id=0, has_side_effects=True),
    )(x, a, pair_cot, w, bias[None, :])
    grad_w = gw.astype(F32).reshape(C, C, z).transpose(1, 0, 2).reshape(C * C, z)
    keep = mask.astype(F32)
    grad_left = (gl.reshape(rows, samples, C) * keep[:, :, None]).reshape(rows, width)
    grad_right = (gr.reshape(rows, C, samples) * keep[:, None, :]).transpose(0, 2, 1).reshape(rows, width)
    return pu, grad_left, grad_right, grad_w, gb.reshape(z)


def solution(mesh):
    placed = (
        P(("grp", "pi"), None),
        P(("grp", "pi"), None),
        P(("grp", "pi")),
        P(),
        P(),
        P(("grp", "pi"), None, None),
    )
    return jax.shard_map(
        functools.partial(local, mesh.shape["pi"]),
        mesh=mesh,
        in_specs=placed,
        out_specs=(
            P(("grp", "pi"), None, None),
            P(("grp", "pi"), None),
            P(("grp", "pi"), None),
            P("grp", None),
            P("grp"),
        ),
        check_vma=False,
    )
```

```python
import functools

import jax
import jax.numpy as jnp
from jax import lax
from jax.experimental import pallas as pl
from jax.experimental.pallas import tpu as pltpu
from jax.sharding import PartitionSpec as P

C = 32
EPSILON = 0.001
EXTRA = 16
MESH = pl.DeviceIdType.MESH
F32 = jnp.float32
BF16 = jnp.bfloat16


def split(x):
    high = x.astype(BF16)
    return high, (x - high.astype(F32)).astype(BF16)


def mm(x, y):
    return jnp.dot(x, y, preferred_element_type=F32)


def mm_nt(x, y):
    return lax.dot_general(x, y, (((1,), (1,)), ((), ())), preferred_element_type=F32)


def kernel(
    n, x_ref, a_ref, cot_ref, w_ref, bias_ref,
    pu_ref, gl_ref, gr_ref, gw_ref, gb_ref,
    gat, bs, uhi, ulo, t_ref, pair_w, got_w, send_w, recv_w,
    part_r, pair_r, got_r, send_r, recv_r, mine_w, all_w,
    send_sems, recv_sems,
):
    me = lax.axis_index("pi")
    rows = x_ref.shape[0]
    z = w_ref.shape[1]
    width = x_ref.shape[1] - z
    samples = width // C
    total = cot_ref.shape[1]
    chunk = gw_ref.shape[1]

    core = lax.rem(me, 2)
    chip = me // 2
    partner = me + 1 - 2 * core
    chips = n // 2

    def copy(k, source, target, peer, slot, sent):
        return pltpu.make_async_remote_copy(
            src_ref=source, dst_ref=target,
            send_sem=send_sems.at[k, sent], recv_sem=recv_sems.at[k, slot],
            device_id={"pi": peer}, device_id_type=MESH,
        )

    def each(act):
        def body(step, carry):
            act(lax.rem(me + 2 * step, n))
            return carry

        lax.fori_loop(1, chips, body, 0)

    def other(p):
        return p + 1 - 2 * core

    def direct(k, source, target, p):
        return copy(k, source, target.at[me], p, me, p)

    def landed(k, target, p):
        return copy(k, target.at[p], target.at[p], partner, p, other(p))

    def gather_start(k, source, target):
        each(lambda p: direct(k, source, target, p).start())
        direct(k, source, target, partner).start()
        target[me] = source[...]

    def gather_pass(k, target):
        def act(p):
            landed(k, target, p).wait_recv()
            landed(k, target, p).start()

        each(act)

    def gather_end(k, target):
        landed(k, target, partner).wait_recv()
        each(lambda p: landed(k, target, other(p)).wait_recv())

    def gather_sent(k, source, target):
        each(lambda p: direct(k, source, target, p).wait_send())
        direct(k, source, target, partner).wait_send()
        each(lambda p: landed(k, target, p).wait_send())

    def pair(index, source, target):
        return copy(4, source.at[1 - core], target, partner, index, index)

    def across(k, source, target, p):
        return copy(k, source.at[p // 2], target.at[chip], p, me, p)

    def across_in(k, source, target, p):
        return copy(k, source.at[p // 2], target.at[p // 2], p, p, p)

    barrier = pltpu.get_barrier_semaphore()

    def greet(p):
        pl.semaphore_signal(barrier, inc=1, device_id={"pi": p}, device_id_type=MESH)

    each(greet)
    greet(partner)
    pl.semaphore_wait(barrier, chips)
    gather_start(0, x_ref, gat)

    a = a_ref[...]
    for d in range(C):
        high, low = split(mm(a, w_ref[d * C:(d + 1) * C, :]))
        for i in range(rows):
            here = (slice(d * samples, (d + 1) * samples), slice(i * z, (i + 1) * z))
            uhi[here] = high[i * samples:(i + 1) * samples]
            ulo[here] = low[i * samples:(i + 1) * samples]
    a_t = jnp.concatenate([a, a], axis=0).astype(F32).T.astype(BF16)

    gather_pass(0, gat)
    gather_end(0, gat)

    def gather_rows(q, carry):
        both = jnp.concatenate([gat[2 * q].astype(F32), gat[2 * q + 1].astype(F32)], axis=0)
        bs[pl.ds(pl.multiple_of(q * 2 * rows, 2 * rows), 2 * rows), :] = both
        return carry

    lax.fori_loop(0, n // 2, gather_rows, 0)
    b32 = bs[:, :width]
    b = b32.astype(BF16)
    depths = bs[:, width:]
    inverse, highs, lows = [], [], []
    cot_sum = jnp.zeros((1, z), F32)
    for i in range(rows):
        inverse.append(1.0 / (EPSILON + jnp.minimum(depths, x_ref[i:i + 1, width:].astype(F32))))
        cot = cot_ref[i].astype(F32)
        cot_sum = cot_sum + jnp.sum(cot, axis=0, keepdims=True)
        high, low = split(cot * inverse[i])
        highs.append(high)
        lows.append(low)
    cot_high = jnp.concatenate(highs, axis=1)
    cot_low = jnp.concatenate(lows, axis=1)
    b_t = jnp.concatenate([b32, b32], axis=0).T.astype(BF16)
    t_ref[...] = mm(b_t, jnp.concatenate([cot_high, cot_low], axis=0))

    def t_of(d):
        return jnp.concatenate(
            [t_ref[d * samples:(d + 1) * samples, i * z:(i + 1) * z] for i in range(rows)], axis=0
        )

    per = max(1, chunk // C)
    for d in range(C):
        high, low = split(t_of(d))
        piece = mm(a_t, jnp.concatenate([high, low], axis=0))
        if chunk >= C:
            p = d // per
            pair_w[p % 2, p // 2, (d % per) * C:(d % per + 1) * C, :] = piece
        else:
            for k in range(C // chunk):
                p = d * (C // chunk) + k
                pair_w[p % 2, p // 2, :chunk, :] = piece[k * chunk:(k + 1) * chunk]
    sums = jnp.concatenate([cot_sum, jnp.zeros((EXTRA - 1, z), F32)], axis=0)

    def put_sums(m, carry):
        pair_w[0, m, chunk:, :] = sums
        pair_w[1, m, chunk:, :] = sums
        return carry

    lax.fori_loop(0, chips, put_sums, 0)
    pair(0, pair_w, got_w).start()

    u_high = uhi[...]
    part_r[...] = mm_nt(cot_high, u_high) + mm_nt(cot_low, u_high) + mm_nt(cot_high, ulo[...])

    def scatter_rows(q, carry):
        both = part_r[pl.ds(pl.multiple_of(q * 2 * rows, 2 * rows), 2 * rows), :]
        pair_r[0, q] = both[:rows]
        pair_r[1, q] = both[rows:]
        return carry

    lax.fori_loop(0, chips, scatter_rows, 0)
    pair(1, pair_r, got_r).start()

    pair(0, pair_w, got_w).wait_recv()

    def join_w(m, carry):
        both = pair_w[core, m] + got_w[m]
        high, low = split(both[chunk:chunk + 1])
        tail = jnp.concatenate(
            [high.astype(F32), low.astype(F32), jnp.zeros((EXTRA - 2, z), F32)], axis=0
        )
        send_w[m, :chunk, :] = both[:chunk].astype(BF16)
        send_w[m, chunk:, :] = tail.astype(BF16)
        return carry

    lax.fori_loop(0, chips, join_w, 0)
    each(lambda p: across(1, send_w, recv_w, p).start())
    recv_w[chip] = send_w[chip]

    pair(1, pair_r, got_r).wait_recv()

    def join_r(m, carry):
        send_r[m] = (pair_r[core, m] + got_r[m]).astype(BF16)
        return carry

    lax.fori_loop(0, chips, join_r, 0)
    each(lambda p: across(2, send_r, recv_r, p).start())
    recv_r[chip] = send_r[chip]

    update = mm(b, u_high) + mm(b, ulo[...])
    for i in range(rows):
        pu_ref[i] = (update[:, i * z:(i + 1) * z] * inverse[i] + bias_ref[...]).astype(BF16)

    each(lambda p: across_in(1, send_w, recv_w, p).wait_recv())

    def add_w(m, acc):
        return acc + recv_w[m].astype(F32)

    total_w = lax.fori_loop(0, chips, add_w, jnp.zeros((chunk + EXTRA, z), F32))
    mine_w[...] = total_w[:chunk].astype(BF16)
    gb_ref[...] = total_w[chunk:chunk + 1] + total_w[chunk + 1:chunk + 2]
    gather_start(3, mine_w, all_w)

    left_acc = jnp.zeros((rows * samples, C), F32)
    for d in range(C):
        high, low = split(t_of(d))
        w_d = w_ref[d * C:(d + 1) * C, :]
        left_acc = left_acc + mm_nt(
            jnp.concatenate([high, low], axis=1), jnp.concatenate([w_d, w_d], axis=1)
        )
    gl_ref[...] = left_acc

    gather_pass(3, all_w)
    each(lambda p: across_in(2, send_r, recv_r, p).wait_recv())

    def add_r(m, acc):
        return acc + recv_r[m].astype(F32)

    gr_ref[...] = lax.fori_loop(0, chips, add_r, jnp.zeros((rows, width), F32))

    gather_end(3, all_w)
    gw_ref[...] = all_w[...]
    gather_sent(0, x_ref, gat)
    gather_sent(3, mine_w, all_w)
    pair(0, pair_w, got_w).wait_send()
    pair(1, pair_r, got_r).wait_send()
    each(lambda p: across(1, send_w, recv_w, p).wait_send())
    each(lambda p: across(2, send_r, recv_r, p).wait_send())


def local(n, left, right, depth, w_out, bias, pair_cot):
    rows, width = left.shape
    samples = width // C
    total, z = pair_cot.shape[1:]
    chunk = w_out.shape[0] // n
    mask = jnp.arange(samples, dtype=jnp.int32)[None, :] < depth[:, None]
    own = mask.astype(BF16)[:, :, None]
    a = (left.reshape(rows, samples, C) * own).reshape(rows * samples, C)
    b = (right.reshape(rows, samples, C) * own).transpose(0, 2, 1).reshape(rows, width)
    x = jnp.concatenate([b, jnp.broadcast_to(depth.astype(BF16)[:, None], (rows, z))], axis=1)
    w = w_out.reshape(C, C, z).transpose(1, 0, 2).reshape(C * C, z)
    vmem = pl.BlockSpec(memory_space=pltpu.VMEM)
    pu, gl, gr, gw, gb = pl.pallas_call(
        functools.partial(kernel, n),
        out_shape=(
            jax.ShapeDtypeStruct((rows, total, z), BF16),
            jax.ShapeDtypeStruct((rows * samples, C), F32),
            jax.ShapeDtypeStruct((rows, width), F32),
            jax.ShapeDtypeStruct((n, chunk, z), BF16),
            jax.ShapeDtypeStruct((1, z), F32),
        ),
        in_specs=[vmem] * 5,
        out_specs=(vmem,) * 5,
        scratch_shapes=[
            pltpu.VMEM((n, rows, width + z), BF16),
            pltpu.VMEM((total, width + z), F32),
            pltpu.VMEM((C * samples, rows * z), BF16),
            pltpu.VMEM((C * samples, rows * z), BF16),
            pltpu.VMEM((C * samples, rows * z), F32),
            pltpu.VMEM((2, n // 2, chunk + EXTRA, z), F32),
            pltpu.VMEM((n // 2, chunk + EXTRA, z), F32),
            pltpu.VMEM((n // 2, chunk + EXTRA, z), BF16),
            pltpu.VMEM((n // 2, chunk + EXTRA, z), BF16),
            pltpu.VMEM((total, width), F32),
            pltpu.VMEM((2, n // 2, rows, width), F32),
            pltpu.VMEM((n // 2, rows, width), F32),
            pltpu.VMEM((n // 2, rows, width), BF16),
            pltpu.VMEM((n // 2, rows, width), BF16),
            pltpu.VMEM((chunk, z), BF16),
            pltpu.VMEM((n, chunk, z), BF16),
            pltpu.SemaphoreType.DMA((5, n)),
            pltpu.SemaphoreType.DMA((5, n)),
        ],
        compiler_params=pltpu.CompilerParams(collective_id=0, has_side_effects=True),
    )(x, a, pair_cot, w, bias[None, :])
    grad_w = gw.astype(F32).reshape(C, C, z).transpose(1, 0, 2).reshape(C * C, z)
    keep = mask.astype(F32)
    grad_left = (gl.reshape(rows, samples, C) * keep[:, :, None]).reshape(rows, width)
    grad_right = (gr.reshape(rows, C, samples) * keep[:, None, :]).transpose(0, 2, 1).reshape(rows, width)
    return pu, grad_left, grad_right, grad_w, gb.reshape(z)


def solution(mesh):
    placed = (
        P(("grp", "pi"), None),
        P(("grp", "pi"), None),
        P(("grp", "pi")),
        P(),
        P(),
        P(("grp", "pi"), None, None),
    )
    return jax.shard_map(
        functools.partial(local, mesh.shape["pi"]),
        mesh=mesh,
        in_specs=placed,
        out_specs=(
            P(("grp", "pi"), None, None),
            P(("grp", "pi"), None),
            P(("grp", "pi"), None),
            P("grp", None),
            P("grp"),
        ),
        check_vma=False,
    )
```

```python
import functools

import jax
import jax.numpy as jnp
from jax import lax
from jax.experimental import pallas as pl
from jax.experimental.pallas import tpu as pltpu
from jax.sharding import PartitionSpec as P

C = 32
EPSILON = 0.001
EXTRA = 16
MESH = pl.DeviceIdType.MESH
F32 = jnp.float32
BF16 = jnp.bfloat16


def split(x):
    high = x.astype(BF16)
    return high, (x - high.astype(F32)).astype(BF16)


def mm(x, y):
    return jnp.dot(x, y, preferred_element_type=F32)


def mm_nt(x, y):
    return lax.dot_general(x, y, (((1,), (1,)), ((), ())), preferred_element_type=F32)


def kernel(
    n, left_ref, right_ref, depth_ref, cot_ref, w_in, bias_ref,
    pu_ref, gl_ref, gr_ref, gw_ref, gb_ref,
    x_ref, w_ref, u_ref, gw_part, gat, bs, uhi, ulo, t_ref, pair_w, got_w, send_w, recv_w,
    part_r, pair_r, got_r, send_r, recv_r, mine_w, all_w,
    send_sems, recv_sems,
):
    me = lax.axis_index("pi")
    rows, width = right_ref.shape
    z = w_in.shape[1]
    samples = width // C
    total = cot_ref.shape[1]
    chunk = gw_ref.shape[1]

    core = lax.rem(me, 2)
    chip = me // 2
    partner = me + 1 - 2 * core
    chips = n // 2

    def copy(k, source, target, peer, slot, sent):
        return pltpu.make_async_remote_copy(
            src_ref=source, dst_ref=target,
            send_sem=send_sems.at[k, sent], recv_sem=recv_sems.at[k, slot],
            device_id={"pi": peer}, device_id_type=MESH,
        )

    def each(act):
        def body(step, carry):
            act(lax.rem(me + 2 * step, n))
            return carry

        lax.fori_loop(1, chips, body, 0)

    def other(p):
        return p + 1 - 2 * core

    def direct(k, source, target, p):
        return copy(k, source, target.at[me], p, me, p)

    def landed(k, target, p):
        return copy(k, target.at[p], target.at[p], partner, p, other(p))

    def gather_start(k, source, target):
        each(lambda p: direct(k, source, target, p).start())
        direct(k, source, target, partner).start()
        target[me] = source[...]

    def gather_pass(k, target):
        def act(p):
            landed(k, target, p).wait_recv()
            landed(k, target, p).start()

        each(act)

    def gather_end(k, target):
        landed(k, target, partner).wait_recv()
        each(lambda p: landed(k, target, other(p)).wait_recv())

    def gather_sent(k, source, target):
        each(lambda p: direct(k, source, target, p).wait_send())
        direct(k, source, target, partner).wait_send()
        each(lambda p: landed(k, target, p).wait_send())

    def pair(index, source, target):
        return copy(4, source.at[1 - core], target, partner, index, index)

    def across(k, source, target, p):
        return copy(k, source.at[p // 2], target.at[chip], p, me, p)

    def across_in(k, source, target, p):
        return copy(k, source.at[p // 2], target.at[p // 2], p, p, p)

    barrier = pltpu.get_barrier_semaphore()

    def greet(p):
        pl.semaphore_signal(barrier, inc=1, device_id={"pi": p}, device_id_type=MESH)

    each(greet)
    greet(partner)
    spot = (rows, rows)
    wide = jnp.broadcast_to(depth_ref[...], spot).astype(F32)
    diagonal = lax.broadcasted_iota(jnp.int32, spot, 0) == lax.broadcasted_iota(jnp.int32, spot, 1)
    own_depth = jnp.sum(jnp.where(diagonal, wide, 0.0), axis=1, keepdims=True)
    x_ref[:, :width] = right_ref[...]
    x_ref[:, width:] = jnp.broadcast_to(own_depth, (rows, z)).astype(BF16)
    pl.semaphore_wait(barrier, chips)
    gather_start(0, x_ref, gat)

    def sample_of(count):
        return lax.broadcasted_iota(jnp.int32, (count, width), 1) // C

    def kept(count, depths):
        return sample_of(count).astype(F32) < depths

    line = lax.broadcasted_iota(jnp.int32, (samples, width), 0)
    diagonal = sample_of(samples) == line
    own_lines = [
        diagonal & (line.astype(F32) < jnp.broadcast_to(own_depth[i:i + 1], (samples, width)))
        for i in range(rows)
    ]
    fold = (
        lax.broadcasted_iota(jnp.int32, (width, C), 0) % C
        == lax.broadcasted_iota(jnp.int32, (width, C), 1)
    ).astype(F32).astype(BF16)
    unfold = (
        lax.broadcasted_iota(jnp.int32, (C, width), 1) % C
        == lax.broadcasted_iota(jnp.int32, (C, width), 0)
    ).astype(F32).astype(BF16)
    left = left_ref[...].astype(F32)
    spread = [
        jnp.where(own_lines[i], jnp.broadcast_to(left[i:i + 1], (samples, width)), 0.0)
        for i in range(rows)
    ]
    a32 = mm(jnp.concatenate(spread, axis=0).astype(BF16), fold)
    a = a32.astype(BF16)
    w_ref[...] = w_in[...].astype(F32)

    def w_of(d):
        return w_ref[pl.ds(d, C, stride=C), :].astype(BF16)

    for d in range(C):
        product = mm(a, w_of(d))
        for i in range(rows):
            u_ref[pl.ds(i * width + d, samples, stride=C), :] = product[i * samples:(i + 1) * samples]
    for i in range(rows):
        high, low = split(u_ref[i * width:(i + 1) * width])
        uhi[:, i * z:(i + 1) * z] = high
        ulo[:, i * z:(i + 1) * z] = low
    a_t = jnp.concatenate([a32, a32], axis=0).T.astype(BF16)

    gather_pass(0, gat)
    gather_end(0, gat)

    def gather_rows(q, carry):
        both = jnp.concatenate([gat[2 * q].astype(F32), gat[2 * q + 1].astype(F32)], axis=0)
        bs[pl.ds(pl.multiple_of(q * 2 * rows, 2 * rows), 2 * rows), :] = both
        return carry

    lax.fori_loop(0, n // 2, gather_rows, 0)
    depths = bs[:, width:]
    b32 = jnp.where(
        kept(total, jnp.concatenate([depths] * (width // z), axis=1)), bs[:, :width], 0.0
    )
    b = b32.astype(BF16)
    inverse, highs, lows = [], [], []
    cot_sum = jnp.zeros((1, z), F32)
    for i in range(rows):
        inverse.append(1.0 / (EPSILON + jnp.minimum(depths, own_depth[i:i + 1])))
        cot = cot_ref[i].astype(F32)
        cot_sum = cot_sum + jnp.sum(cot, axis=0, keepdims=True)
        high, low = split(cot * inverse[i])
        highs.append(high)
        lows.append(low)
    cot_high = jnp.concatenate(highs, axis=1)
    cot_low = jnp.concatenate(lows, axis=1)
    b_t = jnp.concatenate([b32, b32], axis=0).T.astype(BF16)
    t = mm(b_t, jnp.concatenate([cot_high, cot_low], axis=0))
    for i in range(rows):
        t_ref[i * width:(i + 1) * width, :] = t[:, i * z:(i + 1) * z]

    def t_of(d):
        return jnp.concatenate(
            [t_ref[pl.ds(i * width + d, samples, stride=C), :] for i in range(rows)], axis=0
        )

    for d in range(C):
        high, low = split(t_of(d))
        gw_part[pl.ds(d, C, stride=C), :] = mm(a_t, jnp.concatenate([high, low], axis=0))
    for p in range(n):
        pair_w[p % 2, p // 2, :chunk, :] = gw_part[p * chunk:(p + 1) * chunk]
    sums = jnp.concatenate([cot_sum, jnp.zeros((EXTRA - 1, z), F32)], axis=0)

    def put_sums(m, carry):
        pair_w[0, m, chunk:, :] = sums
        pair_w[1, m, chunk:, :] = sums
        return carry

    lax.fori_loop(0, chips, put_sums, 0)
    pair(0, pair_w, got_w).start()

    u_high = uhi[...]
    part_r[...] = mm_nt(cot_high, u_high) + mm_nt(cot_low, u_high) + mm_nt(cot_high, ulo[...])

    def scatter_rows(q, carry):
        both = part_r[pl.ds(pl.multiple_of(q * 2 * rows, 2 * rows), 2 * rows), :]
        pair_r[0, q] = both[:rows]
        pair_r[1, q] = both[rows:]
        return carry

    lax.fori_loop(0, chips, scatter_rows, 0)
    pair(1, pair_r, got_r).start()

    pair(0, pair_w, got_w).wait_recv()

    def join_w(m, carry):
        both = pair_w[core, m] + got_w[m]
        high, low = split(both[chunk:chunk + 1])
        tail = jnp.concatenate(
            [high.astype(F32), low.astype(F32), jnp.zeros((EXTRA - 2, z), F32)], axis=0
        )
        send_w[m, :chunk, :] = both[:chunk].astype(BF16)
        send_w[m, chunk:, :] = tail.astype(BF16)
        return carry

    lax.fori_loop(0, chips, join_w, 0)
    each(lambda p: across(1, send_w, recv_w, p).start())
    recv_w[chip] = send_w[chip]

    pair(1, pair_r, got_r).wait_recv()

    def join_r(m, carry):
        send_r[m] = (pair_r[core, m] + got_r[m]).astype(BF16)
        return carry

    lax.fori_loop(0, chips, join_r, 0)
    each(lambda p: across(2, send_r, recv_r, p).start())
    recv_r[chip] = send_r[chip]

    update = mm(b, u_high) + mm(b, ulo[...])
    for i in range(rows):
        pu_ref[i] = (update[:, i * z:(i + 1) * z] * inverse[i] + bias_ref[...]).astype(BF16)

    each(lambda p: across_in(1, send_w, recv_w, p).wait_recv())

    def add_w(m, acc):
        return acc + recv_w[m].astype(F32)

    total_w = lax.fori_loop(0, chips, add_w, jnp.zeros((chunk + EXTRA, z), F32))
    mine_w[...] = total_w[:chunk].astype(BF16)
    gb_ref[...] = total_w[chunk:chunk + 1] + total_w[chunk + 1:chunk + 2]
    gather_start(3, mine_w, all_w)

    left_acc = jnp.zeros((rows * samples, C), F32)
    for d in range(C):
        high, low = split(t_of(d))
        w_d = w_of(d)
        left_acc = left_acc + mm_nt(
            jnp.concatenate([high, low], axis=1), jnp.concatenate([w_d, w_d], axis=1)
        )
    high, low = split(left_acc)
    lines = mm(high, unfold) + mm(low, unfold)
    for i in range(rows):
        gl_ref[i:i + 1, :] = jnp.sum(
            jnp.where(own_lines[i], lines[i * samples:(i + 1) * samples], 0.0), axis=0, keepdims=True
        )

    gather_pass(3, all_w)
    each(lambda p: across_in(2, send_r, recv_r, p).wait_recv())

    def add_r(m, acc):
        return acc + recv_r[m].astype(F32)

    total_r = lax.fori_loop(0, chips, add_r, jnp.zeros((rows, width), F32))
    gr_ref[...] = jnp.where(kept(rows, jnp.broadcast_to(own_depth, (rows, width))), total_r, 0.0)

    gather_end(3, all_w)
    gw_ref[...] = all_w[...].astype(F32)
    gather_sent(0, x_ref, gat)
    gather_sent(3, mine_w, all_w)
    pair(0, pair_w, got_w).wait_send()
    pair(1, pair_r, got_r).wait_send()
    each(lambda p: across(1, send_w, recv_w, p).wait_send())
    each(lambda p: across(2, send_r, recv_r, p).wait_send())


def local(n, left, right, depth, w_out, bias, pair_cot):
    rows, width = left.shape
    total, z = pair_cot.shape[1:]
    chunk = w_out.shape[0] // n
    vmem = pl.BlockSpec(memory_space=pltpu.VMEM)
    pu, gl, gr, gw, gb = pl.pallas_call(
        functools.partial(kernel, n),
        out_shape=(
            jax.ShapeDtypeStruct((rows, total, z), BF16),
            jax.ShapeDtypeStruct((rows, width), F32),
            jax.ShapeDtypeStruct((rows, width), F32),
            jax.ShapeDtypeStruct((n, chunk, z), F32),
            jax.ShapeDtypeStruct((1, z), F32),
        ),
        in_specs=[vmem] * 6,
        out_specs=(vmem,) * 5,
        scratch_shapes=[
            pltpu.VMEM((rows, width + z), BF16),
            pltpu.VMEM((C * C, z), F32),
            pltpu.VMEM((rows * width, z), F32),
            pltpu.VMEM((C * C, z), F32),
            pltpu.VMEM((n, rows, width + z), BF16),
            pltpu.VMEM((total, width + z), F32),
            pltpu.VMEM((width, rows * z), BF16),
            pltpu.VMEM((width, rows * z), BF16),
            pltpu.VMEM((rows * width, z), F32),
            pltpu.VMEM((2, n // 2, chunk + EXTRA, z), F32),
            pltpu.VMEM((n // 2, chunk + EXTRA, z), F32),
            pltpu.VMEM((n // 2, chunk + EXTRA, z), BF16),
            pltpu.VMEM((n // 2, chunk + EXTRA, z), BF16),
            pltpu.VMEM((total, width), F32),
            pltpu.VMEM((2, n // 2, rows, width), F32),
            pltpu.VMEM((n // 2, rows, width), F32),
            pltpu.VMEM((n // 2, rows, width), BF16),
            pltpu.VMEM((n // 2, rows, width), BF16),
            pltpu.VMEM((chunk, z), BF16),
            pltpu.VMEM((n, chunk, z), BF16),
            pltpu.SemaphoreType.DMA((5, n)),
            pltpu.SemaphoreType.DMA((5, n)),
        ],
        compiler_params=pltpu.CompilerParams(collective_id=0, has_side_effects=True),
    )(left, right, depth[None, :], pair_cot, w_out, bias[None, :])
    return pu, gl, gr, gw.reshape(C * C, z), gb.reshape(z)


def solution(mesh):
    placed = (
        P(("grp", "pi"), None),
        P(("grp", "pi"), None),
        P(("grp", "pi")),
        P(),
        P(),
        P(("grp", "pi"), None, None),
    )
    return jax.shard_map(
        functools.partial(local, mesh.shape["pi"]),
        mesh=mesh,
        in_specs=placed,
        out_specs=(
            P(("grp", "pi"), None, None),
            P(("grp", "pi"), None),
            P(("grp", "pi"), None),
            P("grp", None),
            P("grp"),
        ),
        check_vma=False,
    )
```

```python
import functools

import jax
import jax.numpy as jnp
from jax import lax
from jax.experimental import pallas as pl
from jax.experimental.pallas import tpu as pltpu
from jax.sharding import PartitionSpec as P

C = 32
EPSILON = 0.001
MESH = pl.DeviceIdType.MESH
F32 = jnp.float32
BF16 = jnp.bfloat16


def split(x):
    high = x.astype(BF16)
    return high, (x - high.astype(F32)).astype(BF16)


def mm(x, y):
    return jnp.dot(x, y, preferred_element_type=F32)


def mm_nt(x, y):
    return lax.dot_general(x, y, (((1,), (1,)), ((), ())), preferred_element_type=F32)


def kernel(
    n, left_ref, right_ref, depth_ref, cot_ref, w_in, bias_ref,
    pu_ref, gl_ref, gr_ref, gw_ref, gb_ref,
    x_ref, w_ref, u_ref, gw_part, gat, bs, uhi, ulo, t_ref, pair_w, got_w, send_w, recv_w,
    part_r, pair_r, got_r, send_r, recv_r, mine_w, all_w,
    send_sems, recv_sems,
):
    me = lax.axis_index("pi")
    rows, width = right_ref.shape
    z = w_in.shape[1]
    samples = width // C
    total = cot_ref.shape[1]
    chunk = gw_ref.shape[1]

    core = lax.rem(me, 2)
    chip = me // 2
    partner = me + 1 - 2 * core
    chips = n // 2

    def copy(k, source, target, peer, slot, sent):
        return pltpu.make_async_remote_copy(
            src_ref=source, dst_ref=target,
            send_sem=send_sems.at[k, sent], recv_sem=recv_sems.at[k, slot],
            device_id={"pi": peer}, device_id_type=MESH,
        )

    def each(act):
        def body(step, carry):
            act(lax.rem(me + 2 * step, n))
            return carry

        lax.fori_loop(1, chips, body, 0)

    def other(p):
        return p + 1 - 2 * core

    def direct(k, source, target, p):
        return copy(k, source, target.at[me], p, me, p)

    def landed(k, target, p):
        return copy(k, target.at[p], target.at[p], partner, p, other(p))

    def gather_start(k, source, target):
        each(lambda p: direct(k, source, target, p).start())
        direct(k, source, target, partner).start()
        target[me] = source[...]

    def gather_pass(k, target):
        def act(p):
            landed(k, target, p).wait_recv()
            landed(k, target, p).start()

        each(act)

    def gather_end(k, target):
        landed(k, target, partner).wait_recv()
        each(lambda p: landed(k, target, other(p)).wait_recv())

    def gather_sent(k, source, target):
        each(lambda p: direct(k, source, target, p).wait_send())
        direct(k, source, target, partner).wait_send()
        each(lambda p: landed(k, target, p).wait_send())

    def pair(index, source, target):
        return copy(4, source.at[1 - core], target, partner, index, index)

    def across(k, source, target, p):
        return copy(k, source.at[p // 2], target.at[chip], p, me, p)

    def across_in(k, source, target, p):
        return copy(k, source.at[p // 2], target.at[p // 2], p, p, p)

    barrier = pltpu.get_barrier_semaphore()

    def greet(p):
        pl.semaphore_signal(barrier, inc=1, device_id={"pi": p}, device_id_type=MESH)

    each(greet)
    greet(partner)
    spot = (rows, rows)
    wide = jnp.broadcast_to(depth_ref[...], spot).astype(F32)
    diagonal = lax.broadcasted_iota(jnp.int32, spot, 0) == lax.broadcasted_iota(jnp.int32, spot, 1)
    own_depth = jnp.sum(jnp.where(diagonal, wide, 0.0), axis=1, keepdims=True)
    x_ref[:, :width] = right_ref[...]
    x_ref[:, width:width + z] = jnp.broadcast_to(own_depth, (rows, z)).astype(BF16)
    cot_sum = jnp.zeros((1, z), F32)
    for i in range(rows):
        cot_sum = cot_sum + jnp.sum(cot_ref[i].astype(F32), axis=0, keepdims=True)
    high, low = split(cot_sum)
    x_ref[:, width + z:] = jnp.concatenate(
        [high.astype(F32), low.astype(F32), jnp.zeros((rows - 2, z), F32)], axis=0
    ).astype(BF16)
    pl.semaphore_wait(barrier, chips)
    gather_start(0, x_ref, gat)

    def sample_of(count):
        return lax.broadcasted_iota(jnp.int32, (count, width), 1) // C

    def kept(count, depths):
        return sample_of(count).astype(F32) < depths

    line = lax.broadcasted_iota(jnp.int32, (samples, width), 0)
    diagonal = sample_of(samples) == line
    own_lines = [
        diagonal & (line.astype(F32) < jnp.broadcast_to(own_depth[i:i + 1], (samples, width)))
        for i in range(rows)
    ]
    fold = (
        lax.broadcasted_iota(jnp.int32, (width, C), 0) % C
        == lax.broadcasted_iota(jnp.int32, (width, C), 1)
    ).astype(F32).astype(BF16)
    unfold = (
        lax.broadcasted_iota(jnp.int32, (C, width), 1) % C
        == lax.broadcasted_iota(jnp.int32, (C, width), 0)
    ).astype(F32).astype(BF16)
    left = left_ref[...].astype(F32)
    spread = [
        jnp.where(own_lines[i], jnp.broadcast_to(left[i:i + 1], (samples, width)), 0.0)
        for i in range(rows)
    ]
    a32 = mm(jnp.concatenate(spread, axis=0).astype(BF16), fold)
    a = a32.astype(BF16)
    w_ref[...] = w_in[...].astype(F32)

    def w_of(d):
        return w_ref[pl.ds(d, C, stride=C), :].astype(BF16)

    for d in range(C):
        product = mm(a, w_of(d))
        for i in range(rows):
            u_ref[pl.ds(i * width + d, samples, stride=C), :] = product[i * samples:(i + 1) * samples]
    for i in range(rows):
        high, low = split(u_ref[i * width:(i + 1) * width])
        uhi[:, i * z:(i + 1) * z] = high
        ulo[:, i * z:(i + 1) * z] = low
    a_t = jnp.concatenate([a32, a32], axis=0).T.astype(BF16)

    gather_pass(0, gat)
    gather_end(0, gat)

    def gather_rows(q, carry):
        both = jnp.concatenate([gat[2 * q].astype(F32), gat[2 * q + 1].astype(F32)], axis=0)
        bs[pl.ds(pl.multiple_of(q * 2 * rows, 2 * rows), 2 * rows), :] = both
        return carry

    lax.fori_loop(0, n // 2, gather_rows, 0)
    depths = bs[:, width:width + z]
    gb_ref[...] = jnp.sum(bs[:, width + z:], axis=0, keepdims=True)
    b32 = jnp.where(
        kept(total, jnp.concatenate([depths] * (width // z), axis=1)), bs[:, :width], 0.0
    )
    b = b32.astype(BF16)
    inverse, highs, lows = [], [], []
    for i in range(rows):
        inverse.append(1.0 / (EPSILON + jnp.minimum(depths, own_depth[i:i + 1])))
        cot = cot_ref[i].astype(F32)
        high, low = split(cot * inverse[i])
        highs.append(high)
        lows.append(low)
    cot_high = jnp.concatenate(highs, axis=1)
    cot_low = jnp.concatenate(lows, axis=1)
    b_t = jnp.concatenate([b32, b32], axis=0).T.astype(BF16)
    t = mm(b_t, jnp.concatenate([cot_high, cot_low], axis=0))
    for i in range(rows):
        t_ref[i * width:(i + 1) * width, :] = t[:, i * z:(i + 1) * z]

    def t_of(d):
        return jnp.concatenate(
            [t_ref[pl.ds(i * width + d, samples, stride=C), :] for i in range(rows)], axis=0
        )

    for d in range(C):
        high, low = split(t_of(d))
        gw_part[pl.ds(d, C, stride=C), :] = mm(a_t, jnp.concatenate([high, low], axis=0))
    for p in range(n):
        pair_w[p % 2, p // 2] = gw_part[p * chunk:(p + 1) * chunk]
    pair(0, pair_w, got_w).start()

    u_high = uhi[...]
    part_r[...] = mm_nt(cot_high, u_high) + mm_nt(cot_low, u_high) + mm_nt(cot_high, ulo[...])

    def scatter_rows(q, carry):
        both = part_r[pl.ds(pl.multiple_of(q * 2 * rows, 2 * rows), 2 * rows), :]
        pair_r[0, q] = both[:rows]
        pair_r[1, q] = both[rows:]
        return carry

    lax.fori_loop(0, chips, scatter_rows, 0)
    pair(1, pair_r, got_r).start()

    pair(0, pair_w, got_w).wait_recv()

    def join_w(m, carry):
        send_w[m] = (pair_w[core, m] + got_w[m]).astype(BF16)
        return carry

    lax.fori_loop(0, chips, join_w, 0)
    each(lambda p: across(1, send_w, recv_w, p).start())
    recv_w[chip] = send_w[chip]

    pair(1, pair_r, got_r).wait_recv()

    def join_r(m, carry):
        send_r[m] = (pair_r[core, m] + got_r[m]).astype(BF16)
        return carry

    lax.fori_loop(0, chips, join_r, 0)
    each(lambda p: across(2, send_r, recv_r, p).start())
    recv_r[chip] = send_r[chip]

    update = mm(b, u_high) + mm(b, ulo[...])
    for i in range(rows):
        pu_ref[i] = (update[:, i * z:(i + 1) * z] * inverse[i] + bias_ref[...]).astype(BF16)

    each(lambda p: across_in(1, send_w, recv_w, p).wait_recv())

    def add_w(m, acc):
        return acc + recv_w[m].astype(F32)

    total_w = lax.fori_loop(0, chips, add_w, jnp.zeros((chunk, z), F32))
    mine_w[...] = total_w.astype(BF16)
    gather_start(3, mine_w, all_w)

    left_acc = jnp.zeros((rows * samples, C), F32)
    for d in range(C):
        high, low = split(t_of(d))
        w_d = w_of(d)
        left_acc = left_acc + mm_nt(
            jnp.concatenate([high, low], axis=1), jnp.concatenate([w_d, w_d], axis=1)
        )
    high, low = split(left_acc)
    lines = mm(high, unfold) + mm(low, unfold)
    for i in range(rows):
        gl_ref[i:i + 1, :] = jnp.sum(
            jnp.where(own_lines[i], lines[i * samples:(i + 1) * samples], 0.0), axis=0, keepdims=True
        )

    gather_pass(3, all_w)
    each(lambda p: across_in(2, send_r, recv_r, p).wait_recv())

    def add_r(m, acc):
        return acc + recv_r[m].astype(F32)

    total_r = lax.fori_loop(0, chips, add_r, jnp.zeros((rows, width), F32))
    gr_ref[...] = jnp.where(kept(rows, jnp.broadcast_to(own_depth, (rows, width))), total_r, 0.0)

    gather_end(3, all_w)
    gw_ref[...] = all_w[...]
    gather_sent(0, x_ref, gat)
    gather_sent(3, mine_w, all_w)
    pair(0, pair_w, got_w).wait_send()
    pair(1, pair_r, got_r).wait_send()
    each(lambda p: across(1, send_w, recv_w, p).wait_send())
    each(lambda p: across(2, send_r, recv_r, p).wait_send())


def finish(*refs):
    half = len(refs) // 2
    for source, target in zip(refs[:half], refs[half:]):
        target[...] = source[...].astype(target.dtype)


def local(n, left, right, depth, w_out, bias, pair_cot):
    rows, width = left.shape
    total, z = pair_cot.shape[1:]
    chunk = w_out.shape[0] // n
    vmem = pl.BlockSpec(memory_space=pltpu.VMEM)
    results = pl.pallas_call(
        functools.partial(kernel, n),
        out_shape=(
            jax.ShapeDtypeStruct((rows, total, z), BF16),
            jax.ShapeDtypeStruct((rows, width), F32),
            jax.ShapeDtypeStruct((rows, width), F32),
            jax.ShapeDtypeStruct((n, chunk, z), BF16),
            jax.ShapeDtypeStruct((1, z), F32),
        ),
        in_specs=[vmem] * 6,
        out_specs=(vmem,) * 5,
        scratch_shapes=[
            pltpu.VMEM((rows, width + 2 * z), BF16),
            pltpu.VMEM((C * C, z), F32),
            pltpu.VMEM((rows * width, z), F32),
            pltpu.VMEM((C * C, z), F32),
            pltpu.VMEM((n, rows, width + 2 * z), BF16),
            pltpu.VMEM((total, width + 2 * z), F32),
            pltpu.VMEM((width, rows * z), BF16),
            pltpu.VMEM((width, rows * z), BF16),
            pltpu.VMEM((rows * width, z), F32),
            pltpu.VMEM((2, n // 2, chunk, z), F32),
            pltpu.VMEM((n // 2, chunk, z), F32),
            pltpu.VMEM((n // 2, chunk, z), BF16),
            pltpu.VMEM((n // 2, chunk, z), BF16),
            pltpu.VMEM((total, width), F32),
            pltpu.VMEM((2, n // 2, rows, width), F32),
            pltpu.VMEM((n // 2, rows, width), F32),
            pltpu.VMEM((n // 2, rows, width), BF16),
            pltpu.VMEM((n // 2, rows, width), BF16),
            pltpu.VMEM((chunk, z), BF16),
            pltpu.VMEM((n, chunk, z), BF16),
            pltpu.SemaphoreType.DMA((5, n)),
            pltpu.SemaphoreType.DMA((5, n)),
        ],
        compiler_params=pltpu.CompilerParams(collective_id=0, has_side_effects=True),
    )(left, right, depth[None, :], pair_cot, w_out, bias[None, :])
    pu, gl, gr, gw, gb = pl.pallas_call(
        finish,
        out_shape=tuple(
            jax.ShapeDtypeStruct(r.shape, F32 if k == 3 else r.dtype) for k, r in enumerate(results)
        ),
        in_specs=[vmem] * 5,
        out_specs=(vmem,) * 5,
    )(*results)
    return pu, gl, gr, gw.reshape(C * C, z), gb.reshape(z)


def solution(mesh):
    placed = (
        P(("grp", "pi"), None),
        P(("grp", "pi"), None),
        P(("grp", "pi")),
        P(),
        P(),
        P(("grp", "pi"), None, None),
    )
    return jax.shard_map(
        functools.partial(local, mesh.shape["pi"]),
        mesh=mesh,
        in_specs=placed,
        out_specs=(
            P(("grp", "pi"), None, None),
            P(("grp", "pi"), None),
            P(("grp", "pi"), None),
            P("grp", None),
            P("grp"),
        ),
        check_vma=False,
    )
```
